256 devices in a mesh: cuts: 4 (over x), region: 64 (over z, y, core).
Axes of the slice: x: 4, y: 4, z: 8, core: 2. Of those that a mesh axis runs over, the one named last changes fastest.
Arguments:
- image: float32 [4096, 64, 128], P('region', 'cuts'), may hold values from -6 to 6
- precond: float32 [4096, 64, 128], P('region', 'cuts'), may hold values from 1 to 4
- table: bfloat16 [32, 4, 128, 128], replicated, may hold values from 0 to 0.019897461
- subset: int32 [32], replicated, may hold values from 0 to 31, each once
- tile_pixel: int32 [64, 2048], P('region'), may hold values from 0 to 63
- tile_slot: int32 [64, 2048], P('region'), may hold values from 0 to 127
- send_count: int32 [64, 64], P('region'), may hold values from 1 to 5, 128 in all within a row
- recv_map: int32 [64, 64, 5], replicated, may hold values from 0 to 5
- measured: float32 [384, 64, 128], P('region', 'cuts'), may hold values from -6 to 6
- stat_weight: float32 [384, 64, 128], P('region', 'cuts'), may hold values from 0.25 to 1
Outputs:
- updated: float32 [4096, 64, 128], P('region', 'cuts')
- residual: float32 [384, 64, 128], P('region', 'cuts')
The draws below stay inside these ranges and needn't reach their ends.
Inputs may be any that keep to these rules, and one draw needn't show every extreme that they name: `send_count`: each row sums to 128; a region's slots are laid out by owner, in owner order. `recv_map`: entry [d, r, p] is used only where p < send_count[r, d]. `subset`: A permutation of the 32 tabulated angles.
All inputs are finite; a program needn't handle non-finite values.
Results may differ from the reference program's by a relative error of at most 0.005.
Values may be sent and summed in bfloat16 or wider, within the bound.
No kernel may reach another device: no remote copies, remote signals or barrier semaphores. Data moves between devices by JAX's collectives and lax.ppermute only.
A program may use at most 128 MiB of HBM per device.

```python
import math
import jax
import jax.numpy as jnp
import numpy as np
from jax import lax

TILE = 128
PB = 64
ANG = 16
ANG_ALL = 32
SHIFTS = 4
OWN = 6
CAP = 5
NT = 2048
LOC = 128
RAYBLK = 384
SLICES = 64
PIXBLK = 4096
N_REGION = 64


def place_ends(drawn, rng, least, largest):
    longest = drawn.shape.index(max(drawn.shape))
    spots = []
    for shift in (0, 1):
        where = [jax.random.randint(jax.random.fold_in(rng, axis), (), 0, length) for axis, length in enumerate(drawn.shape)]
        where[longest] = (where[longest] + shift) % drawn.shape[longest]
        spots.append(tuple(where))
    return drawn.at[spots[0]].set(least).at[spots[1]].set(largest)


def steps_of(stream_key, dims, split, least, top_value):
    def one(dim, blocks):
        steps = jax.random.uniform(jax.random.fold_in(jax.random.fold_in(stream_key, 6), dim), (blocks,), jnp.float32, least / len(split), top_value / len(split))
        return jnp.repeat(jnp.exp(steps), dims[dim] // blocks).reshape((-1,) + (1,) * (len(dims) - dim - 1))

    factor_of = one(*split[0])
    for cut in split[1:]:
        factor_of = factor_of * one(*cut)
    return factor_of


def split_up(number_of, total, limit, lean):
    portions = [(1 << 20) // math.isqrt(standing ** lean) + 1 for standing in range(2, number_of + 1)]
    surplus, given = total - limit - (number_of - 1), [1] * (number_of - 1)
    while surplus > 0:
        movable = [i for i in range(number_of - 1) if given[i] < limit]
        whole, budget = sum([portions[i] for i in movable]), surplus
        for i in movable:
            more = min(limit - given[i], max(1, budget * portions[i] // whole), surplus)
            given[i] = given[i] + more
            surplus = surplus - more
    return np.array([limit] + given)


def uneven(stream_key, count, total, most, lean):
    if count == 2:
        one = jax.random.randint(stream_key, (), max(1, total - most), min(most, total - 1) + 1)
        return jnp.stack([one, total - one])
    sizes = jnp.asarray(split_up(count, total, most, lean), jnp.int32)
    couples = (count - 1) // 2
    donor, taker = sizes[1:1 + 2 * couples:2], sizes[2:2 + 2 * couples:2]
    margin = jnp.minimum(donor - 1, most - taker)
    passed = jax.random.randint(jax.random.fold_in(stream_key, 1), (couples,), 0, 1 << 20) % (margin + 1)
    sizes = sizes.at[1:1 + 2 * couples:2].set(donor - passed).at[2:2 + 2 * couples:2].set(taker + passed)
    return sizes[jax.random.permutation(jax.random.fold_in(stream_key, 2), count)]


def normal_values(own_key, shape, spread, most, cuts=(), held_as=jnp.bfloat16):
    array = spread * jax.random.normal(own_key, shape, jnp.float32)
    if cuts:
        array = array * steps_of(own_key, shape, cuts, -0.22, 0.18)
    return jnp.clip(array, -most, most).astype(held_as)


def setup_inputs(seed: int = 0) -> dict:
    key_list = jax.random.split(jax.random.key(seed), 11)
    image = normal_values(key_list[0], (PIXBLK, SLICES, TILE), 1.0, 6.0, ((0, 64), (1, 4)), jnp.float32)
    precond = jnp.clip(jnp.exp(math.log(4.0) - 1.3862944 * jax.random.uniform(key_list[1], (PIXBLK, SLICES, TILE), jnp.float32) ** steps_of(key_list[1], (PIXBLK, SLICES, TILE), ((0, 64), (1, 4)), -0.2, 0.2)), 1.0, 4.0)
    table = jnp.clip(jax.random.uniform(key_list[2], (ANG_ALL, SHIFTS, TILE, TILE), jnp.float32, 0.0, 0.019897461), 0.0, 0.019897461).astype(jnp.bfloat16)
    subset = jax.random.permutation(key_list[3], ANG_ALL).astype(jnp.int32)
    tile_pixel = place_ends(jax.random.randint(key_list[4], (N_REGION, NT), 0, PB), jax.random.fold_in(key_list[4], 1), 0, PB - 1).astype(jnp.int32)
    tile_slot = place_ends(jax.random.randint(key_list[5], (N_REGION, NT), 0, LOC), jax.random.fold_in(key_list[5], 1), 0, LOC - 1).astype(jnp.int32)
    send_count = jax.vmap(lambda own: uneven(own, N_REGION, LOC, CAP, 2))(jax.random.split(key_list[6], N_REGION)).reshape((N_REGION, N_REGION)).astype(jnp.int32)
    recv_map = place_ends(jax.random.randint(key_list[7], (N_REGION, N_REGION, CAP), 0, OWN), jax.random.fold_in(key_list[7], 1), 0, OWN - 1).astype(jnp.int32)
    measured = normal_values(key_list[8], (RAYBLK, SLICES, TILE), 1.0, 6.0, ((0, 64), (1, 4)), jnp.float32)
    stat_weight = jnp.clip(0.25 + 0.75 * jax.random.uniform(key_list[9], (RAYBLK, SLICES, TILE), jnp.float32) ** steps_of(key_list[9], (RAYBLK, SLICES, TILE), ((0, 64), (1, 4)), -0.2, 0.2), 0.25, 1.0)
    return {"image": image, "precond": precond, "table": table, "subset": subset, "tile_pixel": tile_pixel, "tile_slot": tile_slot, "send_count": send_count, "recv_map": recv_map, "measured": measured, "stat_weight": stat_weight}


smoothing_weight = 0.5


def source_geometry(counts, owner_map):
    slot_ends = jnp.cumsum(counts).astype(jnp.int32)
    starts = (slot_ends - counts).astype(jnp.int32)
    slot_index = jnp.arange(LOC, dtype=jnp.int32)
    target = jnp.sum((slot_ends[None, :] <= slot_index[:, None]).astype(jnp.int32), axis=1).astype(jnp.int32)
    position = (slot_index - starts[target]).astype(jnp.int32)
    return (target * OWN + owner_map[target, position]).astype(jnp.int32)


def reference(image, precond, table, subset, tile_pixel, tile_slot, send_count, recv_map, measured, stat_weight):
    footprints = table[subset[:ANG]].reshape(ANG * SHIFTS, TILE, TILE).astype(jnp.float32)
    regions = image.astype(jnp.bfloat16).reshape(N_REGION, PB, SLICES, TILE)
    maps = jnp.transpose(recv_map, (1, 0, 2))

    def forward(running, inputs):
        region_block, tile_pixels, tile_slots, counts, owner_map = inputs
        gathered = region_block[tile_pixels].astype(jnp.float32).reshape(ANG * SHIFTS, PB // 2, SLICES, TILE)
        partial_value = jnp.einsum('kij,ktsj->ktsi', footprints, gathered).reshape(NT, SLICES, TILE)
        local_sums = jax.ops.segment_sum(partial_value, tile_slots, num_segments=LOC)
        ray_ids = source_geometry(counts, owner_map)
        return running + jax.ops.segment_sum(local_sums, ray_ids, num_segments=RAYBLK), None

    start_sum = jnp.zeros((RAYBLK, SLICES, TILE), jnp.float32)
    summed, _ = lax.scan(forward, start_sum, (regions, tile_pixel, tile_slot, send_count, maps))
    residual = stat_weight * (measured - summed)
    resid_half = residual.astype(jnp.bfloat16)

    def backward(inputs):
        tile_pixels, tile_slots, counts, owner_map = inputs
        ray_ids = source_geometry(counts, owner_map)
        slot_rows = resid_half[ray_ids[tile_slots]].astype(jnp.float32).reshape(ANG * SHIFTS, PB // 2, SLICES, TILE)
        back_terms = jnp.einsum('kij,ktsi->ktsj', footprints, slot_rows).reshape(NT, SLICES, TILE)
        return jax.ops.segment_sum(back_terms, tile_pixels, num_segments=PB)

    gradient = lax.map(backward, (tile_pixel, tile_slot, send_count, maps)).reshape(PIXBLK, SLICES, TILE)
    differences = image[:, 1:, :] - image[:, :-1, :]
    smooth = jnp.pad(-differences, ((0, 0), (0, 1), (0, 0))) + jnp.pad(differences, ((0, 0), (1, 0), (0, 0)))
    updated = image + (gradient - smoothing_weight * smooth) / precond
    return updated, residual
```

```python
import functools

import jax
import jax.numpy as jnp
from jax import lax
from jax.experimental import pallas as pl
from jax.experimental.pallas import tpu as pltpu
from jax.sharding import PartitionSpec as P

ANG = 16
SHIFTS = 4
OWN = 6
CAP = 5
NZ, NY, NC = 8, 4, 2
smoothing_weight = 0.5
NACC = 4


def fill_rays(counts, owner_map, place, rays):
    def owner(d, start):
        base = place[d]
        for p in range(CAP):
            rays[start + p] = base + owner_map[d * CAP + p]
        return start + counts[d]

    lax.fori_loop(0, NZ * NY * NC, owner, jnp.int32(0))


def forward_kernel(subset, pixels, slots, counts, owner_map, place, table, image, out, xb, rays, *accs):
    step = pl.program_id(0)
    tiles = pixels.shape[0] // (ANG * SHIFTS)

    @pl.when(step == 0)
    def _():
        fill_rays(counts, owner_map, place, rays)
        xb[...] = image[...].astype(jnp.bfloat16)
        for acc in accs:
            acc[...] = jnp.zeros_like(acc)

    slabs = xb.shape[1]
    for shift in range(SHIFTS):
        base = (step * SHIFTS + shift) * tiles
        x = jnp.concatenate([xb[pixels[base + t]] for t in range(tiles)], axis=0)
        y = lax.dot_general(
            x, table[0, shift], (((1,), (1,)), ((), ())), preferred_element_type=jnp.float32
        )
        for t in range(tiles):
            acc = accs[t % len(accs)]
            row = rays[slots[base + t]]
            acc[row] += y[t * slabs : (t + 1) * slabs]

    @pl.when(step == ANG - 1)
    def _():
        @pl.loop(0, out.shape[0], unroll=4)
        def _(r):
            out[r] = sum(acc[r] for acc in accs).astype(jnp.bfloat16)


def backward_kernel(subset, pixels, slots, counts, owner_map, place, table, mine, theirs, start, precond, out, rb, rays, *accs):
    step = pl.program_id(0)
    tiles = pixels.shape[0] // (ANG * SHIFTS)

    @pl.when(step == 0)
    def _():
        fill_rays(counts, owner_map, place, rays)
        half = mine.shape[0]
        rb[:half] = mine[...]
        rb[half:] = theirs[...]
        for acc in accs:
            acc[...] = jnp.zeros_like(acc)

    slabs = rb.shape[1]
    for shift in range(SHIFTS):
        base = (step * SHIFTS + shift) * tiles
        x = jnp.concatenate([rb[rays[slots[base + t]]] for t in range(tiles)], axis=0)
        y = jnp.dot(x, table[0, shift], preferred_element_type=jnp.float32)
        for t in range(tiles):
            acc = accs[t % len(accs)]
            row = pixels[base + t]
            acc[row] += y[t * slabs : (t + 1) * slabs]

    @pl.when(step == ANG - 1)
    def _():
        @pl.loop(0, out.shape[0], unroll=4)
        def _(r):
            out[r] = start[r] + sum(acc[r] for acc in accs) / precond[r]


def whole(array):
    return pl.BlockSpec(array.shape, lambda a, *_: (0,) * array.ndim)


def table_spec(table):
    return pl.BlockSpec((1,) + table.shape[1:], lambda a, subset, *_: (subset[a], 0, 0, 0))


def call(kernel, name, scalars, table, dense, out, width, rows, flops, bytes_moved):
    slabs, lanes = dense[0].shape[1:]
    return pl.pallas_call(
        kernel,
        name=name,
        out_shape=out,
        grid_spec=pltpu.PrefetchScalarGridSpec(
            num_scalar_prefetch=len(scalars),
            grid=(ANG,),
            in_specs=[table_spec(table)] + [whole(d) for d in dense],
            out_specs=whole(out),
            scratch_shapes=[
                pltpu.VMEM((width, slabs, lanes), jnp.bfloat16),
                pltpu.SMEM((160,), jnp.int32),
            ]
            + [pltpu.VMEM((rows, slabs, lanes), jnp.float32)] * NACC,
        ),
        compiler_params=pltpu.CompilerParams(
            dimension_semantics=("arbitrary",), vmem_limit_bytes=40 << 20
        ),
        cost_estimate=pl.CostEstimate(flops=flops, bytes_accessed=bytes_moved, transcendentals=0),
    )(*scalars, table, *dense)


def index_of(z, y, c):
    return (z * NY + y) * NC + c


GROUP_Y = [[index_of(z, y, c) for y in range(NY)] for z in range(NZ) for c in range(NC)]
GROUP_Z = [[index_of(z, y, c) for z in range(NZ)] for y in range(NY) for c in range(NC)]
SWAP = [(i, i ^ 1) for i in range(NZ * NY * NC)]


def exchange(x, groups):
    return lax.all_to_all(
        x, "region", split_axis=0, concat_axis=0, tiled=True, axis_index_groups=groups
    )


def per_device(
    image, precond, table, subset, tile_pixel, tile_slot, send_count, recv_map, measured, stat_weight
):
    blocks, slabs, lanes = image.shape
    me = lax.axis_index("region")
    core = me % NC
    owners = jnp.arange(NZ * NY * NC, dtype=jnp.int32)
    oz, oy, oc = owners // (NY * NC), owners // NC % NY, owners % NC
    place = (((oc ^ core) * NY + oy) * NZ + oz) * OWN
    owner_map = lax.dynamic_index_in_dim(recv_map, me, 1, keepdims=False).reshape(-1)
    scalars = (subset, tile_pixel[0], tile_slot[0], send_count[0], owner_map, place.astype(jnp.int32))
    rows = NZ * NY * NC * OWN
    half = rows // 2

    cuts = lax.axis_size("cuts")
    up = [(i, i + 1) for i in range(cuts - 1)]
    before = lax.ppermute(image[:, -1:, :], "cuts", up)
    after = lax.ppermute(image[:, :1, :], "cuts", [(j, i) for i, j in up])

    local = call(
        forward_kernel, "project", scalars, table, (image,),
        jax.ShapeDtypeStruct((rows, slabs, lanes), jnp.bfloat16), blocks, rows,
        2 * 2048 * slabs * lanes * lanes, 6 << 20,
    )
    other = lax.ppermute(local[half:], "region", SWAP)
    chip = (local[:half].astype(jnp.float32) + other.astype(jnp.float32)).astype(jnp.bfloat16)
    got = exchange(chip, GROUP_Y).reshape(NY, NZ * OWN, slabs, lanes)
    row = jnp.sum(got.astype(jnp.float32), axis=0).astype(jnp.bfloat16)
    got = exchange(row, GROUP_Z).reshape(NZ, OWN, slabs, lanes)
    summed = jnp.sum(got.astype(jnp.float32), axis=0)
    residual = stat_weight * (measured - summed)
    resid_half = residual.astype(jnp.bfloat16)

    back = exchange(jnp.tile(resid_half, (NZ, 1, 1, 1)).reshape(NZ * OWN, slabs, lanes), GROUP_Z)
    back = lax.all_gather(back, "region", axis=0, tiled=True, axis_index_groups=GROUP_Y)
    theirs = lax.ppermute(back, "region", SWAP)

    padded = jnp.concatenate([before, image, after], axis=1)
    global_slice = lax.axis_index("cuts") * slabs + jnp.arange(slabs, dtype=jnp.int32)
    below = jnp.where((global_slice > 0)[None, :, None], image - padded[:, :-2, :], 0.0)
    above = jnp.where(
        (global_slice < slabs * cuts - 1)[None, :, None], image - padded[:, 2:, :], 0.0
    )
    start = image - smoothing_weight * (below + above) / precond
    updated = call(
        backward_kernel, "backproject", scalars, table, (back, theirs, start, precond),
        jax.ShapeDtypeStruct(image.shape, jnp.float32), rows, blocks,
        2 * 2048 * slabs * lanes * lanes, 6 << 20,
    )
    return (updated, residual)


def solution(mesh):
    in_specs = (
        P("region", "cuts", None),
        P("region", "cuts", None),
        P(),
        P(),
        P("region", None),
        P("region", None),
        P("region", None),
        P(),
        P("region", "cuts", None),
        P("region", "cuts", None),
    )
    out_specs = (P("region", "cuts", None), P("region", "cuts", None))
    return jax.shard_map(
        per_device, mesh=mesh, in_specs=in_specs, out_specs=out_specs, check_vma=False
    )
```

```python
import jax
import jax.numpy as jnp
from jax import lax
from jax.experimental import pallas as pl
from jax.experimental.pallas import tpu as pltpu
from jax.sharding import PartitionSpec as P

ANG = 16
SHIFTS = 4
OWN = 6
CAP = 5
NZ, NY, NC = 8, 4, 2
smoothing_weight = 0.5
NACC = 4
WINDOWS = 4
VMEM = 48 << 20
LOC = 128
SLABS = 16
LANES = 128


def fill_rays(counts, owner_rows, rays):
    def owner(d, start):
        for p in range(CAP):
            rays[start + p] = owner_rows[p, d]
        return start + counts[0, d]

    lax.fori_loop(0, NZ * NY * NC, owner, jnp.int32(0))


class Tables:
    def __init__(self, pixels, slots, counts, owner_rows, subset, table, scratch):
        (self.counts_s, self.owner_s, self.subset_s, self.rays, self.table_v,
         self.sems, self.table_sems, self.window_sems) = scratch[:8]
        self.windows = [scratch[8 + 2 * b : 10 + 2 * b] for b in range(WINDOWS)]
        self.pixels, self.slots, self.table = pixels, slots, table
        self.small = [
            pltpu.make_async_copy(source, target, self.sems.at[i])
            for i, (source, target) in enumerate(
                ((subset, self.subset_s), (counts, self.counts_s), (owner_rows, self.owner_s))
            )
        ]

    def window(self, a, b):
        here = pl.ds(pl.multiple_of(a * LANES, LANES), LANES)
        return [
            pltpu.make_async_copy(source.at[:, here], target, self.window_sems.at[i, b])
            for i, (source, target) in enumerate(zip((self.pixels, self.slots), self.windows[b]))
        ]

    def footprints(self, row, a):
        return pltpu.make_async_copy(self.table.at[row], self.table_v.at[a], self.table_sems.at[a])

    def start(self, cleared):
        for copy in self.small:
            copy.start()
        for b in range(WINDOWS):
            for copy in self.window(b, b):
                copy.start()
        for ref in cleared:
            ref[...] = jnp.zeros_like(ref)
        self.small[0].wait()
        for a in range(ANG):
            self.footprints(self.subset_s[a], a).start()
        self.small[1].wait()
        self.small[2].wait()
        fill_rays(self.counts_s, self.owner_s, self.rays)

    def sweep(self, source, accs, take_slot, contract):
        tiles = LANES // SHIFTS

        @pl.loop(0, ANG // WINDOWS)
        def _(g):
            for b in range(WINDOWS):
                a = g * WINDOWS + b
                for copy in self.window(a, b):
                    copy.wait()
                self.footprints(0, a).wait()
                pixel, slot = self.windows[b]
                take, put = (slot, pixel) if take_slot else (pixel, slot)
                for shift in range(SHIFTS):
                    base = shift * tiles
                    x = jnp.concatenate([source[take[0, base + t]] for t in range(tiles)], axis=0)
                    y = lax.dot_general(
                        x, self.table_v[a, shift], (((1,), (contract,)), ((), ())),
                        preferred_element_type=jnp.float32,
                    )
                    for t in range(tiles):
                        acc = accs[t % NACC]
                        acc[put[0, base + t]] += y[t * SLABS : (t + 1) * SLABS]

                @pl.when(g < ANG // WINDOWS - 1)
                def _():
                    for copy in self.window(a + WINDOWS, b):
                        copy.start()


def forward_kernel(pixels, slots, counts, owner_rows, subset, table, image, mine, theirs, low, high, *scratch):
    image_v, xb, total, image_sem = scratch[:4]
    accs = scratch[4 : 4 + NACC]
    tables = Tables(pixels, slots, counts, owner_rows, subset, table, scratch[4 + NACC :])
    image_copy = pltpu.make_async_copy(image, image_v, image_sem)
    image_copy.start()
    tables.start((*accs, total))
    image_copy.wait()
    xb[...] = image_v[...].astype(jnp.bfloat16)
    low[...] = image_v[:, :1, :]
    high[...] = image_v[:, SLABS - 1 :, :]
    tables.sweep(xb, accs, False, 1)

    @pl.loop(0, LOC, unroll=8)
    def _(j):
        total[tables.rays[j]] += sum(acc[j] for acc in accs)

    half = mine.shape[0]
    mine[...] = total[:half].astype(jnp.bfloat16)
    theirs[...] = total[half:].astype(jnp.bfloat16)


def backward_kernel(pixels, slots, counts, owner_rows, subset, table, mine, theirs, start, precond, out, *scratch):
    rb, slot_resid = scratch[:2]
    accs = scratch[2 : 2 + NACC]
    tables = Tables(pixels, slots, counts, owner_rows, subset, table, scratch[2 + NACC :])
    tables.start(accs)
    half = mine.shape[0]
    rb[:half] = mine[...]
    rb[half:] = theirs[...]

    @pl.loop(0, LOC, unroll=8)
    def _(j):
        slot_resid[j] = rb[tables.rays[j]]

    tables.sweep(slot_resid, accs, True, 0)
    out[...] = start[...] + sum(acc[...] for acc in accs) / precond[...]


VM = pl.BlockSpec(memory_space=pltpu.VMEM)
ANYWHERE = pl.BlockSpec(memory_space=pltpu.HBM)


def call(kernel, name, operands, specs, out, dense, acc_rows, flops, bytes_moved):
    table = operands[5]
    several = isinstance(out, (tuple, list))
    return pl.pallas_call(
        kernel,
        name=name,
        out_shape=out,
        in_specs=[ANYWHERE] * 6 + specs,
        out_specs=[VM] * len(out) if several else VM,
        scratch_shapes=dense
        + [pltpu.VMEM((acc_rows, SLABS, LANES), jnp.float32)] * NACC
        + [pltpu.SMEM(operand.shape, jnp.int32) for operand in operands[2:5]]
        + [
            pltpu.SMEM((160,), jnp.int32),
            pltpu.VMEM((ANG,) + table.shape[1:], table.dtype),
            pltpu.SemaphoreType.DMA((3,)),
            pltpu.SemaphoreType.DMA((ANG,)),
            pltpu.SemaphoreType.DMA((2, WINDOWS)),
        ]
        + [pltpu.SMEM((1, LANES), jnp.int32)] * (2 * WINDOWS),
        compiler_params=pltpu.CompilerParams(vmem_limit_bytes=VMEM),
        cost_estimate=pl.CostEstimate(flops=flops, bytes_accessed=bytes_moved, transcendentals=0),
    )(*[
        pltpu.with_memory_space_constraint(operand, pltpu.HBM) if pinned else operand
        for operand, pinned in zip(operands, [i != 3 for i in range(6)] + [s is ANYWHERE for s in specs])
    ])


def index_of(z, y, c):
    return (z * NY + y) * NC + c


GROUP_Y = [[index_of(z, y, c) for y in range(NY)] for z in range(NZ) for c in range(NC)]
GROUP_Z = [[index_of(z, y, c) for z in range(NZ)] for y in range(NY) for c in range(NC)]
SWAP = [(i, i ^ 1) for i in range(NZ * NY * NC)]


def exchange(x, groups):
    return lax.all_to_all(
        x, "region", split_axis=0, concat_axis=0, tiled=True, axis_index_groups=groups
    )


def per_device(
    image, precond, table, subset, tile_pixel, tile_slot, send_count, recv_map, measured, stat_weight
):
    blocks, slabs, lanes = image.shape
    me = lax.axis_index("region")
    core = me % NC
    owners = jnp.arange(NZ * NY * NC, dtype=jnp.int32)
    oz, oy, oc = owners // (NY * NC), owners // NC % NY, owners % NC
    place = (((oc ^ core) * NY + oy) * NZ + oz) * OWN
    mine = jnp.arange(NZ * NY * NC, dtype=jnp.int32) == me
    owner_rows = place[None, :] + jnp.sum(
        jnp.where(mine[None, None, :], recv_map.transpose(2, 0, 1), 0), axis=2
    )
    tables = (tile_pixel, tile_slot, send_count, owner_rows.astype(jnp.int32), subset, table)
    rows = NZ * NY * NC * OWN
    half = rows // 2

    local = jax.ShapeDtypeStruct((half, slabs, lanes), jnp.bfloat16)
    edge = jax.ShapeDtypeStruct((blocks, 1, lanes), jnp.float32)
    kept, given, low, high = call(
        forward_kernel, "project", tables + (image,), [ANYWHERE], (local, local, edge, edge),
        [
            pltpu.VMEM((blocks, slabs, lanes), jnp.float32),
            pltpu.VMEM((blocks, slabs, lanes), jnp.bfloat16),
            pltpu.VMEM((rows, slabs, lanes), jnp.float32),
            pltpu.SemaphoreType.DMA,
        ],
        LOC, 2 * 2048 * slabs * lanes * lanes, 6 << 20,
    )
    cuts = lax.axis_size("cuts")
    up = [(i, i + 1) for i in range(cuts - 1)]
    other = lax.ppermute(given, "region", SWAP)
    before = lax.ppermute(high, "cuts", up)
    after = lax.ppermute(low, "cuts", [(j, i) for i, j in up])
    chip = (kept.astype(jnp.float32) + other.astype(jnp.float32)).astype(jnp.bfloat16)
    got = exchange(chip, GROUP_Y).reshape(NY, NZ * OWN, slabs, lanes)
    row = jnp.sum(got.astype(jnp.float32), axis=0).astype(jnp.bfloat16)
    row, before, after = lax.optimization_barrier((row, before, after))
    got = exchange(row, GROUP_Z).reshape(NZ, OWN, slabs, lanes)
    summed = jnp.sum(got.astype(jnp.float32), axis=0)
    residual = stat_weight * (measured - summed)
    resid_half = residual.astype(jnp.bfloat16)

    back = exchange(jnp.tile(resid_half, (NZ, 1, 1, 1)).reshape(NZ * OWN, slabs, lanes), GROUP_Z)
    back = lax.all_gather(back, "region", axis=0, tiled=True, axis_index_groups=GROUP_Y)
    theirs = lax.ppermute(back, "region", SWAP)

    padded = jnp.concatenate([before, image, after], axis=1)
    global_slice = lax.axis_index("cuts") * slabs + jnp.arange(slabs, dtype=jnp.int32)
    below = jnp.where((global_slice > 0)[None, :, None], image - padded[:, :-2, :], 0.0)
    above = jnp.where(
        (global_slice < slabs * cuts - 1)[None, :, None], image - padded[:, 2:, :], 0.0
    )
    start = image - smoothing_weight * (below + above) / precond
    updated = call(
        backward_kernel, "backproject", tables + (back, theirs, start, precond), [VM] * 4,
        jax.ShapeDtypeStruct(image.shape, jnp.float32),
        [
            pltpu.VMEM((rows, slabs, lanes), jnp.bfloat16),
            pltpu.VMEM((LOC, slabs, lanes), jnp.bfloat16),
        ],
        blocks, 2 * 2048 * slabs * lanes * lanes, 6 << 20,
    )
    return (updated, residual)


def solution(mesh):
    in_specs = (
        P("region", "cuts", None),
        P("region", "cuts", None),
        P(),
        P(),
        P("region", None),
        P("region", None),
        P("region", None),
        P(),
        P("region", "cuts", None),
        P("region", "cuts", None),
    )
    out_specs = (P("region", "cuts", None), P("region", "cuts", None))
    return jax.shard_map(
        per_device, mesh=mesh, in_specs=in_specs, out_specs=out_specs, check_vma=False
    )
```

```python
import jax
import jax.numpy as jnp
from jax import lax
from jax.experimental import pallas as pl
from jax.experimental.pallas import tpu as pltpu
from jax.sharding import PartitionSpec as P

ANG = 16
SHIFTS = 4
OWN = 6
CAP = 5
NZ, NY, NC = 8, 4, 2
smoothing_weight = 0.5
NACC = 6
WINDOWS = 8
TOGETHER = 4
VMEM = 48 << 20
LOC = 128
SLABS = 16
LANES = 128


def fill_rays(counts, owner_rows, rays):
    def owner(d, start):
        for p in range(CAP):
            rays[start + p] = owner_rows[p, d]
        return start + counts[0, d]

    lax.fori_loop(0, NZ * NY * NC, owner, jnp.int32(0))


class Tables:
    def __init__(self, pixels, slots, counts, owner_rows, subset, table, scratch):
        (self.counts_s, self.owner_s, self.subset_s, self.rays, self.table_v,
         self.sems, self.table_sems, self.window_sems, pixels_v, slots_v) = scratch[:10]
        self.staged = (pixels_v, slots_v)
        self.windows = [scratch[10 + 2 * b : 12 + 2 * b] for b in range(WINDOWS)]
        self.table = table
        self.small = [
            pltpu.make_async_copy(source, target, self.sems.at[i])
            for i, (source, target) in enumerate(
                (
                    (subset, self.subset_s), (pixels, pixels_v), (slots, slots_v),
                    (counts, self.counts_s), (owner_rows, self.owner_s),
                )
            )
        ]

    def window(self, a, b):
        here = pl.ds(pl.multiple_of(a * LANES, LANES), LANES)
        return [
            pltpu.make_async_copy(source.at[:, here], target, self.window_sems.at[i, b])
            for i, (source, target) in enumerate(zip(self.staged, self.windows[b]))
        ]

    def footprints(self, row, a):
        return pltpu.make_async_copy(self.table.at[row], self.table_v.at[a], self.table_sems.at[a])

    def start(self, cleared):
        for copy in self.small:
            copy.start()
        half = len(cleared) // 2
        for ref in cleared[:half]:
            ref[...] = jnp.zeros_like(ref)
        self.small[0].wait()
        for a in range(ANG):
            self.footprints(self.subset_s[a], a).start()
        for copy, ref in zip(self.small[1:3], self.staged):
            copy.wait()
            ref[...] = ref[...] * SLABS
        for ref in cleared[half:]:
            ref[...] = jnp.zeros_like(ref)
        for b in range(WINDOWS):
            for copy in self.window(b, b):
                copy.start()
        self.small[3].wait()
        self.small[4].wait()
        fill_rays(self.counts_s, self.owner_s, self.rays)

    def sweep(self, source, accs, take_slot, contract):
        tiles = LANES // SHIFTS

        @pl.loop(0, ANG // WINDOWS)
        def _(g):
            for first in range(0, WINDOWS, TOGETHER):
                turn = range(first, first + TOGETHER)
                for b in turn:
                    for copy in self.window(g * WINDOWS + b, b):
                        copy.wait()
                    self.footprints(0, g * WINDOWS + b).wait()
                for b in turn:
                    pixel, slot = self.windows[b]
                    take, put = (slot, pixel) if take_slot else (pixel, slot)
                    for shift in range(SHIFTS):
                        base = shift * tiles
                        x = jnp.concatenate(
                            [source[pl.ds(take[0, base + t], SLABS), :] for t in range(tiles)], axis=0
                        ).astype(jnp.bfloat16)
                        y = lax.dot_general(
                            x, self.table_v[g * WINDOWS + b, shift],
                            (((1,), (contract,)), ((), ())), preferred_element_type=jnp.float32,
                        )
                        for t in range(tiles):
                            acc = accs[t % NACC]
                            acc[pl.ds(put[0, base + t], SLABS), :] += y[t * SLABS : (t + 1) * SLABS]

                @pl.when(g < ANG // WINDOWS - 1)
                def _():
                    for b in turn:
                        for copy in self.window((g + 1) * WINDOWS + b, b):
                            copy.start()


def forward_kernel(pixels, slots, counts, owner_rows, subset, table, image, mine, theirs, low, high, *scratch):
    image_v, xb, total, image_sem = scratch[:4]
    accs = scratch[4 : 4 + NACC]
    tables = Tables(pixels, slots, counts, owner_rows, subset, table, scratch[4 + NACC :])
    image_copy = pltpu.make_async_copy(image, image_v, image_sem)
    image_copy.start()
    tables.start((*accs, total))
    image_copy.wait()
    xb[...] = image_v[...].astype(jnp.bfloat16).astype(jnp.float32).reshape(xb.shape)
    low[...] = image_v[:, :1, :]
    high[...] = image_v[:, SLABS - 1 :, :]
    tables.sweep(xb, accs, False, 1)

    @pl.loop(0, LOC, unroll=8)
    def _(j):
        here = pl.ds(pl.multiple_of(j * SLABS, SLABS), SLABS)
        total[tables.rays[j]] += sum(acc[here, :] for acc in accs)

    half = mine.shape[0]
    mine[...] = total[:half].astype(jnp.bfloat16)
    theirs[...] = total[half:].astype(jnp.bfloat16)


def backward_kernel(pixels, slots, counts, owner_rows, subset, table, mine, theirs, start, precond, out, *scratch):
    rb, slot_resid = scratch[:2]
    accs = scratch[2 : 2 + NACC]
    tables = Tables(pixels, slots, counts, owner_rows, subset, table, scratch[2 + NACC :])
    tables.start(accs)
    half = mine.shape[0]
    rb[:half] = mine[...]
    rb[half:] = theirs[...]

    @pl.loop(0, LOC, unroll=8)
    def _(j):
        here = pl.ds(pl.multiple_of(j * SLABS, SLABS), SLABS)
        slot_resid[here, :] = rb[tables.rays[j]].astype(jnp.float32)

    tables.sweep(slot_resid, accs, True, 0)
    out[...] = start[...] + sum(acc[...] for acc in accs).reshape(out.shape) / precond[...]


VM = pl.BlockSpec(memory_space=pltpu.VMEM)
ANYWHERE = pl.BlockSpec(memory_space=pltpu.HBM)


def call(kernel, name, operands, specs, out, dense, acc_rows, flops, bytes_moved):
    table = operands[5]
    several = isinstance(out, (tuple, list))
    return pl.pallas_call(
        kernel,
        name=name,
        out_shape=out,
        in_specs=[ANYWHERE] * 6 + specs,
        out_specs=[VM] * len(out) if several else VM,
        scratch_shapes=dense
        + [pltpu.VMEM((acc_rows * SLABS, LANES), jnp.float32)] * NACC
        + [pltpu.SMEM(operand.shape, jnp.int32) for operand in operands[2:5]]
        + [
            pltpu.SMEM((160,), jnp.int32),
            pltpu.VMEM((ANG,) + table.shape[1:], table.dtype),
            pltpu.SemaphoreType.DMA((5,)),
            pltpu.SemaphoreType.DMA((ANG,)),
            pltpu.SemaphoreType.DMA((2, WINDOWS)),
            pltpu.VMEM(operands[0].shape, jnp.int32),
            pltpu.VMEM(operands[1].shape, jnp.int32),
        ]
        + [pltpu.SMEM((1, LANES), jnp.int32)] * (2 * WINDOWS),
        compiler_params=pltpu.CompilerParams(vmem_limit_bytes=VMEM),
        cost_estimate=pl.CostEstimate(flops=flops, bytes_accessed=bytes_moved, transcendentals=0),
    )(*[
        pltpu.with_memory_space_constraint(operand, pltpu.HBM) if pinned else operand
        for operand, pinned in zip(operands, [i != 3 for i in range(6)] + [s is ANYWHERE for s in specs])
    ])


def index_of(z, y, c):
    return (z * NY + y) * NC + c


GROUP_Y = [[index_of(z, y, c) for y in range(NY)] for z in range(NZ) for c in range(NC)]
GROUP_Z = [[index_of(z, y, c) for z in range(NZ)] for y in range(NY) for c in range(NC)]
SWAP = [(i, i ^ 1) for i in range(NZ * NY * NC)]


def exchange(x, groups):
    return lax.all_to_all(
        x, "region", split_axis=0, concat_axis=0, tiled=True, axis_index_groups=groups
    )


def per_device(
    image, precond, table, subset, tile_pixel, tile_slot, send_count, recv_map, measured, stat_weight
):
    blocks, slabs, lanes = image.shape
    me = lax.axis_index("region")
    core = me % NC
    owners = jnp.arange(NZ * NY * NC, dtype=jnp.int32)
    oz, oy, oc = owners // (NY * NC), owners // NC % NY, owners % NC
    place = (((oc ^ core) * NY + oy) * NZ + oz) * OWN
    mine = jnp.arange(NZ * NY * NC, dtype=jnp.int32) == me
    owner_rows = place[None, :] + jnp.sum(
        jnp.where(mine[None, None, :], recv_map.transpose(2, 0, 1), 0), axis=2
    )
    tables = (tile_pixel, tile_slot, send_count, owner_rows.astype(jnp.int32), subset, table)
    rows = NZ * NY * NC * OWN
    half = rows // 2

    local = jax.ShapeDtypeStruct((half, slabs, lanes), jnp.bfloat16)
    edge = jax.ShapeDtypeStruct((blocks, 1, lanes), jnp.float32)
    kept, given, low, high = call(
        forward_kernel, "project", tables + (image,), [ANYWHERE], (local, local, edge, edge),
        [
            pltpu.VMEM((blocks, slabs, lanes), jnp.float32),
            pltpu.VMEM((blocks * slabs, lanes), jnp.float32),
            pltpu.VMEM((rows, slabs, lanes), jnp.float32),
            pltpu.SemaphoreType.DMA,
        ],
        LOC, 2 * 2048 * slabs * lanes * lanes, 6 << 20,
    )
    cuts = lax.axis_size("cuts")
    up = [(i, i + 1) for i in range(cuts - 1)]
    other = lax.ppermute(given, "region", SWAP)
    before = lax.ppermute(high, "cuts", up)
    after = lax.ppermute(low, "cuts", [(j, i) for i, j in up])
    chip = (kept.astype(jnp.float32) + other.astype(jnp.float32)).astype(jnp.bfloat16)
    got = exchange(chip, GROUP_Y).reshape(NY, NZ * OWN, slabs, lanes)
    row = jnp.sum(got.astype(jnp.float32), axis=0).astype(jnp.bfloat16)
    row, before, after = lax.optimization_barrier((row, before, after))
    got = exchange(row, GROUP_Z).reshape(NZ, OWN, slabs, lanes)
    summed = jnp.sum(got.astype(jnp.float32), axis=0)
    residual = stat_weight * (measured - summed)
    resid_half = residual.astype(jnp.bfloat16)

    back = exchange(jnp.tile(resid_half, (NZ, 1, 1, 1)).reshape(NZ * OWN, slabs, lanes), GROUP_Z)
    back = lax.all_gather(back, "region", axis=0, tiled=True, axis_index_groups=GROUP_Y)
    theirs = lax.ppermute(back, "region", SWAP)

    padded = jnp.concatenate([before, image, after], axis=1)
    global_slice = lax.axis_index("cuts") * slabs + jnp.arange(slabs, dtype=jnp.int32)
    below = jnp.where((global_slice > 0)[None, :, None], image - padded[:, :-2, :], 0.0)
    above = jnp.where(
        (global_slice < slabs * cuts - 1)[None, :, None], image - padded[:, 2:, :], 0.0
    )
    start = image - smoothing_weight * (below + above) / precond
    updated = call(
        backward_kernel, "backproject", tables + (back, theirs, start, precond), [VM] * 4,
        jax.ShapeDtypeStruct(image.shape, jnp.float32),
        [
            pltpu.VMEM((rows, slabs, lanes), jnp.bfloat16),
            pltpu.VMEM((LOC * slabs, lanes), jnp.float32),
        ],
        blocks, 2 * 2048 * slabs * lanes * lanes, 6 << 20,
    )
    return (updated, residual)


def solution(mesh):
    in_specs = (
        P("region", "cuts", None),
        P("region", "cuts", None),
        P(),
        P(),
        P("region", None),
        P("region", None),
        P("region", None),
        P(),
        P("region", "cuts", None),
        P("region", "cuts", None),
    )
    out_specs = (P("region", "cuts", None), P("region", "cuts", None))
    return jax.shard_map(
        per_device, mesh=mesh, in_specs=in_specs, out_specs=out_specs, check_vma=False
    )
```

```python
import jax
import jax.numpy as jnp
from jax import lax
from jax.experimental import pallas as pl
from jax.experimental.pallas import tpu as pltpu
from jax.sharding import PartitionSpec as P

ANG = 16
SHIFTS = 4
OWN = 6
CAP = 5
NZ, NY, NC = 8, 4, 2
smoothing_weight = 0.5
NACC = 6
WINDOWS = 8
TOGETHER = 4
VMEM = 48 << 20
LOC = 128
SLABS = 16
LANES = 128


def fill_rays(counts, owner_rows, rays):
    def owner(d, start):
        for p in range(CAP):
            rays[start + p] = owner_rows[p, d]
        return start + counts[0, d]

    lax.fori_loop(0, NZ * NY * NC, owner, jnp.int32(0))


class Tables:
    def __init__(self, pixels, slots, counts, owner_rows, subset, table, scratch):
        (self.counts_s, self.owner_s, self.subset_s, self.rays, self.table_v,
         self.sems, self.table_sems, self.window_sems, pixels_v, slots_v) = scratch[:10]
        self.staged = (pixels_v, slots_v)
        self.windows = [scratch[10 + 2 * b : 12 + 2 * b] for b in range(WINDOWS)]
        self.table = table
        self.small = [
            pltpu.make_async_copy(source, target, self.sems.at[i])
            for i, (source, target) in enumerate(
                (
                    (subset, self.subset_s), (pixels, pixels_v), (slots, slots_v),
                    (counts, self.counts_s), (owner_rows, self.owner_s),
                )
            )
        ]

    def window(self, a, b):
        here = pl.ds(pl.multiple_of(a * LANES, LANES), LANES)
        return [
            pltpu.make_async_copy(source.at[:, here], target, self.window_sems.at[i, b])
            for i, (source, target) in enumerate(zip(self.staged, self.windows[b]))
        ]

    def footprints(self, row, a):
        return pltpu.make_async_copy(self.table.at[row], self.table_v.at[a], self.table_sems.at[a])

    def start(self, cleared):
        for copy in self.small:
            copy.start()
        half = len(cleared) // 2
        for ref in cleared[:half]:
            ref[...] = jnp.zeros_like(ref)
        self.small[0].wait()
        for a in range(ANG):
            self.footprints(self.subset_s[a], a).start()
        for copy, ref in zip(self.small[1:3], self.staged):
            copy.wait()
            ref[...] = ref[...] * SLABS
        for ref in cleared[half:]:
            ref[...] = jnp.zeros_like(ref)
        for b in range(WINDOWS):
            for copy in self.window(b, b):
                copy.start()
        self.small[3].wait()
        self.small[4].wait()
        fill_rays(self.counts_s, self.owner_s, self.rays)

    def sweep(self, source, accs, take_slot, contract):
        tiles = LANES // SHIFTS

        @pl.loop(0, ANG // WINDOWS)
        def _(g):
            for first in range(0, WINDOWS, TOGETHER):
                turn = range(first, first + TOGETHER)
                for b in turn:
                    for copy in self.window(g * WINDOWS + b, b):
                        copy.wait()
                    self.footprints(0, g * WINDOWS + b).wait()
                for b in turn:
                    pixel, slot = self.windows[b]
                    take, put = (slot, pixel) if take_slot else (pixel, slot)
                    for shift in range(SHIFTS):
                        base = shift * tiles
                        x = jnp.concatenate(
                            [source[pl.ds(take[0, base + t], SLABS), :] for t in range(tiles)], axis=0
                        ).astype(jnp.bfloat16)
                        y = lax.dot_general(
                            x, self.table_v[g * WINDOWS + b, shift],
                            (((1,), (contract,)), ((), ())), preferred_element_type=jnp.float32,
                        )
                        for t in range(tiles):
                            acc = accs[t % NACC]
                            acc[pl.ds(put[0, base + t], SLABS), :] += y[t * SLABS : (t + 1) * SLABS]

                @pl.when(g < ANG // WINDOWS - 1)
                def _():
                    for b in turn:
                        for copy in self.window((g + 1) * WINDOWS + b, b):
                            copy.start()


def forward_kernel(pixels, slots, counts, owner_rows, subset, table, image, mine, theirs, low, high, *scratch):
    image_v, xb, total, image_sem = scratch[:4]
    accs = scratch[4 : 4 + NACC]
    tables = Tables(pixels, slots, counts, owner_rows, subset, table, scratch[4 + NACC :])
    image_copy = pltpu.make_async_copy(image, image_v, image_sem)
    image_copy.start()
    tables.start((*accs, total))
    image_copy.wait()
    xb[...] = image_v[...].astype(jnp.bfloat16).astype(jnp.float32).reshape(xb.shape)
    low[...] = image_v[:, :1, :]
    high[...] = image_v[:, SLABS - 1 :, :]
    tables.sweep(xb, accs, False, 1)

    @pl.loop(0, LOC, unroll=8)
    def _(j):
        here = pl.ds(pl.multiple_of(j * SLABS, SLABS), SLABS)
        total[tables.rays[j]] += sum(acc[here, :] for acc in accs)

    half = mine.shape[0]
    mine[...] = total[:half].astype(jnp.bfloat16)
    theirs[...] = total[half:].astype(jnp.bfloat16)


def backward_kernel(pixels, slots, counts, owner_rows, subset, table, mine, theirs, start, precond, out, *scratch):
    rb, slot_resid = scratch[:2]
    accs = scratch[2 : 2 + NACC]
    tables = Tables(pixels, slots, counts, owner_rows, subset, table, scratch[2 + NACC :])
    tables.start(accs)
    half = mine.shape[0]
    rb[:half] = mine[...]
    rb[half:] = theirs[...]

    @pl.loop(0, LOC, unroll=8)
    def _(j):
        here = pl.ds(pl.multiple_of(j * SLABS, SLABS), SLABS)
        slot_resid[here, :] = rb[tables.rays[j]].astype(jnp.float32)

    tables.sweep(slot_resid, accs, True, 0)
    out[...] = start[...] + sum(acc[...] for acc in accs).reshape(out.shape) / precond[...]


VM = pl.BlockSpec(memory_space=pltpu.VMEM)
ANYWHERE = pl.BlockSpec(memory_space=pltpu.HBM)


def call(kernel, name, operands, specs, out, dense, acc_rows, flops, bytes_moved):
    table = operands[5]
    several = isinstance(out, (tuple, list))
    return pl.pallas_call(
        kernel,
        name=name,
        out_shape=out,
        in_specs=[ANYWHERE] * 6 + specs,
        out_specs=[VM] * len(out) if several else VM,
        scratch_shapes=dense
        + [pltpu.VMEM((acc_rows * SLABS, LANES), jnp.float32)] * NACC
        + [pltpu.SMEM(operand.shape, jnp.int32) for operand in operands[2:5]]
        + [
            pltpu.SMEM((160,), jnp.int32),
            pltpu.VMEM((ANG,) + table.shape[1:], table.dtype),
            pltpu.SemaphoreType.DMA((5,)),
            pltpu.SemaphoreType.DMA((ANG,)),
            pltpu.SemaphoreType.DMA((2, WINDOWS)),
            pltpu.VMEM(operands[0].shape, jnp.int32),
            pltpu.VMEM(operands[1].shape, jnp.int32),
        ]
        + [pltpu.SMEM((1, LANES), jnp.int32)] * (2 * WINDOWS),
        compiler_params=pltpu.CompilerParams(vmem_limit_bytes=VMEM),
        cost_estimate=pl.CostEstimate(flops=flops, bytes_accessed=bytes_moved, transcendentals=0),
    )(*[
        pltpu.with_memory_space_constraint(operand, pltpu.HBM) if pinned else operand
        for operand, pinned in zip(operands, [i != 3 for i in range(6)] + [s is ANYWHERE for s in specs])
    ])


def index_of(z, y, c):
    return (z * NY + y) * NC + c


NL = 2
NH = NZ // NL
GROUP_Y = [
    [index_of(h * NL + l, y, c) for y in range(NY) for l in range(NL)]
    for h in range(NH) for c in range(NC)
]
GROUP_Z = [
    [index_of(h * NL + l, y, c) for h in range(NH)]
    for l in range(NL) for y in range(NY) for c in range(NC)
]
SWAP = [(i, i ^ 1) for i in range(NZ * NY * NC)]


def exchange(x, groups):
    return lax.all_to_all(
        x, "region", split_axis=0, concat_axis=0, tiled=True, axis_index_groups=groups
    )


def per_device(
    image, precond, table, subset, tile_pixel, tile_slot, send_count, recv_map, measured, stat_weight
):
    blocks, slabs, lanes = image.shape
    me = lax.axis_index("region")
    core = me % NC
    owners = jnp.arange(NZ * NY * NC, dtype=jnp.int32)
    oz, oy, oc = owners // (NY * NC), owners // NC % NY, owners % NC
    place = ((((oc ^ core) * NY + oy) * NL + oz % NL) * NH + oz // NL) * OWN
    mine = jnp.arange(NZ * NY * NC, dtype=jnp.int32) == me
    owner_rows = place[None, :] + jnp.sum(
        jnp.where(mine[None, None, :], recv_map.transpose(2, 0, 1), 0), axis=2
    )
    tables = (tile_pixel, tile_slot, send_count, owner_rows.astype(jnp.int32), subset, table)
    rows = NZ * NY * NC * OWN
    half = rows // 2

    local = jax.ShapeDtypeStruct((half, slabs, lanes), jnp.bfloat16)
    edge = jax.ShapeDtypeStruct((blocks, 1, lanes), jnp.float32)
    kept, given, low, high = call(
        forward_kernel, "project", tables + (image,), [ANYWHERE], (local, local, edge, edge),
        [
            pltpu.VMEM((blocks, slabs, lanes), jnp.float32),
            pltpu.VMEM((blocks * slabs, lanes), jnp.float32),
            pltpu.VMEM((rows, slabs, lanes), jnp.float32),
            pltpu.SemaphoreType.DMA,
        ],
        LOC, 2 * 2048 * slabs * lanes * lanes, 6 << 20,
    )
    cuts = lax.axis_size("cuts")
    up = [(i, i + 1) for i in range(cuts - 1)]
    other = lax.ppermute(given, "region", SWAP)
    before = lax.ppermute(high, "cuts", up)
    after = lax.ppermute(low, "cuts", [(j, i) for i, j in up])
    chip = (kept.astype(jnp.float32) + other.astype(jnp.float32)).astype(jnp.bfloat16)
    got = exchange(chip, GROUP_Y).reshape(NY * NL, NH * OWN, slabs, lanes)
    row = jnp.sum(got.astype(jnp.float32), axis=0).astype(jnp.bfloat16)
    row, before, after = lax.optimization_barrier((row, before, after))
    got = exchange(row, GROUP_Z).reshape(NH, OWN, slabs, lanes)
    summed = jnp.sum(got.astype(jnp.float32), axis=0)
    residual = stat_weight * (measured - summed)
    resid_half = residual.astype(jnp.bfloat16)

    back = exchange(jnp.tile(resid_half, (NH, 1, 1)), GROUP_Z)
    back = exchange(jnp.tile(back, (NY * NL, 1, 1)), GROUP_Y)
    theirs = lax.ppermute(back, "region", SWAP)

    padded = jnp.concatenate([before, image, after], axis=1)
    global_slice = lax.axis_index("cuts") * slabs + jnp.arange(slabs, dtype=jnp.int32)
    below = jnp.where((global_slice > 0)[None, :, None], image - padded[:, :-2, :], 0.0)
    above = jnp.where(
        (global_slice < slabs * cuts - 1)[None, :, None], image - padded[:, 2:, :], 0.0
    )
    start = image - smoothing_weight * (below + above) / precond
    updated = call(
        backward_kernel, "backproject", tables + (back, theirs, start, precond), [VM] * 4,
        jax.ShapeDtypeStruct(image.shape, jnp.float32),
        [
            pltpu.VMEM((rows, slabs, lanes), jnp.bfloat16),
            pltpu.VMEM((LOC * slabs, lanes), jnp.float32),
        ],
        blocks, 2 * 2048 * slabs * lanes * lanes, 6 << 20,
    )
    return (updated, residual)


def solution(mesh):
    in_specs = (
        P("region", "cuts", None),
        P("region", "cuts", None),
        P(),
        P(),
        P("region", None),
        P("region", None),
        P("region", None),
        P(),
        P("region", "cuts", None),
        P("region", "cuts", None),
    )
    out_specs = (P("region", "cuts", None), P("region", "cuts", None))
    return jax.shard_map(
        per_device, mesh=mesh, in_specs=in_specs, out_specs=out_specs, check_vma=False
    )
```

```python
import jax
import jax.numpy as jnp
from jax import lax
from jax.experimental import pallas as pl
from jax.experimental.pallas import tpu as pltpu
from jax.sharding import PartitionSpec as P

ANG = 16
SHIFTS = 4
OWN = 6
CAP = 5
NZ, NY, NC = 8, 4, 2
smoothing_weight = 0.5
NACC = 6
WINDOWS = 16
TOGETHER = 8
VMEM = 48 << 20
LOC = 128
SLABS = 16
LANES = 128


def fill_rays(counts, owner_rows, rays):
    def owner(d, start):
        for p in range(CAP):
            rays[start + p] = owner_rows[p, d]
        return start + counts[0, d]

    lax.fori_loop(0, NZ * NY * NC, owner, jnp.int32(0))


class Tables:
    def __init__(self, pixels, slots, counts, owner_rows, subset, table, scratch):
        (self.counts_s, self.owner_s, self.subset_s, self.rays, self.table_v,
         self.sems, self.table_sems, self.window_sems, pixels_v, slots_v) = scratch[:10]
        self.staged = (pixels_v, slots_v)
        self.windows = [scratch[10 + 2 * b : 12 + 2 * b] for b in range(WINDOWS)]
        self.table = table
        self.small = [
            pltpu.make_async_copy(source, target, self.sems.at[i])
            for i, (source, target) in enumerate(
                (
                    (subset, self.subset_s), (pixels, pixels_v), (slots, slots_v),
                    (counts, self.counts_s), (owner_rows, self.owner_s),
                )
            )
        ]

    def window(self, a, b):
        here = pl.ds(pl.multiple_of(a * LANES, LANES), LANES)
        return [
            pltpu.make_async_copy(source.at[:, here], target, self.window_sems.at[i, b])
            for i, (source, target) in enumerate(zip(self.staged, self.windows[b]))
        ]

    def footprints(self, row, a):
        return pltpu.make_async_copy(self.table.at[row], self.table_v.at[a], self.table_sems.at[a])

    def start(self, cleared):
        for copy in self.small:
            copy.start()
        half = len(cleared) // 2
        for ref in cleared[:half]:
            ref[...] = jnp.zeros_like(ref)
        self.small[0].wait()
        for a in range(ANG):
            self.footprints(self.subset_s[a], a).start()
        for copy, ref in zip(self.small[1:3], self.staged):
            copy.wait()
            ref[...] = ref[...] * SLABS
        for ref in cleared[half:]:
            ref[...] = jnp.zeros_like(ref)
        for b in range(WINDOWS):
            for copy in self.window(b, b):
                copy.start()
        self.small[3].wait()
        self.small[4].wait()
        fill_rays(self.counts_s, self.owner_s, self.rays)

    def sweep(self, source, accs, take_slot, contract):
        tiles = LANES // SHIFTS

        @pl.loop(0, ANG // WINDOWS)
        def _(g):
            for first in range(0, WINDOWS, TOGETHER):
                turn = range(first, first + TOGETHER)
                for b in turn:
                    for copy in self.window(g * WINDOWS + b, b):
                        copy.wait()
                    self.footprints(0, g * WINDOWS + b).wait()
                for b in turn:
                    pixel, slot = self.windows[b]
                    take, put = (slot, pixel) if take_slot else (pixel, slot)
                    for shift in range(SHIFTS):
                        base = shift * tiles
                        x = jnp.concatenate(
                            [source[pl.ds(take[0, base + t], SLABS), :] for t in range(tiles)], axis=0
                        ).astype(jnp.bfloat16)
                        y = lax.dot_general(
                            x, self.table_v[g * WINDOWS + b, shift],
                            (((1,), (contract,)), ((), ())), preferred_element_type=jnp.float32,
                        )
                        for t in range(tiles):
                            acc = accs[t % NACC]
                            acc[pl.ds(put[0, base + t], SLABS), :] += y[t * SLABS : (t + 1) * SLABS]

                @pl.when(g < ANG // WINDOWS - 1)
                def _():
                    for b in turn:
                        for copy in self.window((g + 1) * WINDOWS + b, b):
                            copy.start()


def forward_kernel(pixels, slots, counts, owner_rows, subset, table, image, mine, theirs, low, high, *scratch):
    image_v, xb, total, image_sem = scratch[:4]
    accs = scratch[4 : 4 + NACC]
    tables = Tables(pixels, slots, counts, owner_rows, subset, table, scratch[4 + NACC :])
    image_copy = pltpu.make_async_copy(image, image_v, image_sem)
    image_copy.start()
    tables.start((*accs, total))
    image_copy.wait()
    xb[...] = image_v[...].astype(jnp.bfloat16).astype(jnp.float32).reshape(xb.shape)
    low[...] = image_v[:, :1, :]
    high[...] = image_v[:, SLABS - 1 :, :]
    tables.sweep(xb, accs, False, 1)

    @pl.loop(0, LOC, unroll=8)
    def _(j):
        here = pl.ds(pl.multiple_of(j * SLABS, SLABS), SLABS)
        total[tables.rays[j]] += sum(acc[here, :] for acc in accs)

    half = mine.shape[0]
    mine[...] = total[:half].astype(jnp.bfloat16)
    theirs[...] = total[half:].astype(jnp.bfloat16)


def backward_kernel(pixels, slots, counts, owner_rows, subset, table, mine, theirs, start, precond, out, *scratch):
    rb, slot_resid = scratch[:2]
    accs = scratch[2 : 2 + NACC]
    tables = Tables(pixels, slots, counts, owner_rows, subset, table, scratch[2 + NACC :])
    tables.start(accs)
    half = mine.shape[0]
    rb[:half] = mine[...]
    rb[half:] = theirs[...]

    @pl.loop(0, LOC, unroll=8)
    def _(j):
        here = pl.ds(pl.multiple_of(j * SLABS, SLABS), SLABS)
        slot_resid[here, :] = rb[tables.rays[j]].astype(jnp.float32)

    tables.sweep(slot_resid, accs, True, 0)
    out[...] = start[...] + sum(acc[...] for acc in accs).reshape(out.shape) / precond[...]


VM = pl.BlockSpec(memory_space=pltpu.VMEM)
ANYWHERE = pl.BlockSpec(memory_space=pltpu.HBM)


def call(kernel, name, operands, specs, out, dense, acc_rows, flops, bytes_moved):
    table = operands[5]
    several = isinstance(out, (tuple, list))
    return pl.pallas_call(
        kernel,
        name=name,
        out_shape=out,
        in_specs=[ANYWHERE] * 6 + specs,
        out_specs=[VM] * len(out) if several else VM,
        scratch_shapes=dense
        + [pltpu.VMEM((acc_rows * SLABS, LANES), jnp.float32)] * NACC
        + [pltpu.SMEM(operand.shape, jnp.int32) for operand in operands[2:5]]
        + [
            pltpu.SMEM((160,), jnp.int32),
            pltpu.VMEM((ANG,) + table.shape[1:], table.dtype),
            pltpu.SemaphoreType.DMA((5,)),
            pltpu.SemaphoreType.DMA((ANG,)),
            pltpu.SemaphoreType.DMA((2, WINDOWS)),
            pltpu.VMEM(operands[0].shape, jnp.int32),
            pltpu.VMEM(operands[1].shape, jnp.int32),
        ]
        + [pltpu.SMEM((1, LANES), jnp.int32)] * (2 * WINDOWS),
        compiler_params=pltpu.CompilerParams(vmem_limit_bytes=VMEM),
        cost_estimate=pl.CostEstimate(flops=flops, bytes_accessed=bytes_moved, transcendentals=0),
    )(*[
        pltpu.with_memory_space_constraint(operand, pltpu.HBM) if pinned else operand
        for operand, pinned in zip(operands, [i != 3 for i in range(6)] + [s is ANYWHERE for s in specs])
    ])


def index_of(z, y, c):
    return (z * NY + y) * NC + c


NL = 2
NH = NZ // NL
GROUP_Y = [
    [index_of(h * NL + l, y, c) for y in range(NY) for l in range(NL)]
    for h in range(NH) for c in range(NC)
]
GROUP_Z = [
    [index_of(h * NL + l, y, c) for h in range(NH)]
    for l in range(NL) for y in range(NY) for c in range(NC)
]
SWAP = [(i, i ^ 1) for i in range(NZ * NY * NC)]


def exchange(x, groups):
    return lax.all_to_all(
        x, "region", split_axis=0, concat_axis=0, tiled=True, axis_index_groups=groups
    )


def per_device(
    image, precond, table, subset, tile_pixel, tile_slot, send_count, recv_map, measured, stat_weight
):
    blocks, slabs, lanes = image.shape
    me = lax.axis_index("region")
    core = me % NC
    owners = jnp.arange(NZ * NY * NC, dtype=jnp.int32)
    oz, oy, oc = owners // (NY * NC), owners // NC % NY, owners % NC
    place = ((((oc ^ core) * NY + oy) * NL + oz % NL) * NH + oz // NL) * OWN
    mine = jnp.arange(NZ * NY * NC, dtype=jnp.int32) == me
    owner_rows = place[None, :] + jnp.sum(
        jnp.where(mine[None, None, :], recv_map.transpose(2, 0, 1), 0), axis=2
    )
    tables = (tile_pixel, tile_slot, send_count, owner_rows.astype(jnp.int32), subset, table)
    rows = NZ * NY * NC * OWN
    half = rows // 2

    local = jax.ShapeDtypeStruct((half, slabs, lanes), jnp.bfloat16)
    edge = jax.ShapeDtypeStruct((blocks, 1, lanes), jnp.float32)
    kept, given, low, high = call(
        forward_kernel, "project", tables + (image,), [ANYWHERE], (local, local, edge, edge),
        [
            pltpu.VMEM((blocks, slabs, lanes), jnp.float32),
            pltpu.VMEM((blocks * slabs, lanes), jnp.float32),
            pltpu.VMEM((rows, slabs, lanes), jnp.float32),
            pltpu.SemaphoreType.DMA,
        ],
        LOC, 2 * 2048 * slabs * lanes * lanes, 6 << 20,
    )
    cuts = lax.axis_size("cuts")
    up = [(i, i + 1) for i in range(cuts - 1)]
    other = lax.ppermute(given, "region", SWAP)
    before = lax.ppermute(high, "cuts", up)
    after = lax.ppermute(low, "cuts", [(j, i) for i, j in up])
    chip = (kept.astype(jnp.float32) + other.astype(jnp.float32)).astype(jnp.bfloat16)
    got = exchange(chip, GROUP_Y).reshape(NY * NL, NH * OWN, slabs, lanes)
    row = jnp.sum(got.astype(jnp.float32), axis=0).astype(jnp.bfloat16)
    row, before, after = lax.optimization_barrier((row, before, after))
    got = exchange(row, GROUP_Z).reshape(NH, OWN, slabs, lanes)
    summed = jnp.sum(got.astype(jnp.float32), axis=0)
    residual = stat_weight * (measured - summed)
    resid_half = residual.astype(jnp.bfloat16)

    back = exchange(jnp.tile(resid_half, (NH, 1, 1)), GROUP_Z)
    back = exchange(jnp.tile(back, (NY * NL, 1, 1)), GROUP_Y)
    theirs = lax.ppermute(back, "region", SWAP)

    padded = jnp.concatenate([before, image, after], axis=1)
    global_slice = lax.axis_index("cuts") * slabs + jnp.arange(slabs, dtype=jnp.int32)
    below = jnp.where((global_slice > 0)[None, :, None], image - padded[:, :-2, :], 0.0)
    above = jnp.where(
        (global_slice < slabs * cuts - 1)[None, :, None], image - padded[:, 2:, :], 0.0
    )
    start = image - smoothing_weight * (below + above) / precond
    updated = call(
        backward_kernel, "backproject", tables + (back, theirs, start, precond), [VM] * 4,
        jax.ShapeDtypeStruct(image.shape, jnp.float32),
        [
            pltpu.VMEM((rows, slabs, lanes), jnp.bfloat16),
            pltpu.VMEM((LOC * slabs, lanes), jnp.float32),
        ],
        blocks, 2 * 2048 * slabs * lanes * lanes, 6 << 20,
    )
    return (updated, residual)


def solution(mesh):
    in_specs = (
        P("region", "cuts", None),
        P("region", "cuts", None),
        P(),
        P(),
        P("region", None),
        P("region", None),
        P("region", None),
        P(),
        P("region", "cuts", None),
        P("region", "cuts", None),
    )
    out_specs = (P("region", "cuts", None), P("region", "cuts", None))
    return jax.shard_map(
        per_device, mesh=mesh, in_specs=in_specs, out_specs=out_specs, check_vma=False
    )
```
